32 devices in a mesh: replica: 2 (over y), fsdp: 4 (over z), tensor: 4 (over x, core).
Axes of the slice: x: 2, y: 2, z: 4, core: 2. Of those that a mesh axis runs over, the one named last changes fastest.
Arguments:
- tokens: bfloat16 [24576, 1024], P(('replica', 'fsdp', 'tensor')), may hold values from -6 to 6
- ln1_gain: float32 [1024], P(('fsdp', 'tensor')), may hold values from 0.5 to 1.5
- ln1_bias: float32 [1024], P(('fsdp', 'tensor')), may hold values from -3 to 3
- qkv_weight: bfloat16 [1024, 3, 1024], P('fsdp', None, 'tensor'), may hold values from -0.1875 to 0.1875
- qv_bias: bfloat16 [2, 16, 64], P(None, 'tensor', 'fsdp'), may hold values from -3 to 3
- out_weight: bfloat16 [1024, 1024], P('tensor', 'fsdp'), may hold values from -0.75 to 0.75
- out_bias: float32 [1024], P(('fsdp', 'tensor')), may hold values from -3 to 3
- ln2_gain: float32 [1024], P(('fsdp', 'tensor')), may hold values from 0.5 to 1.5
- ln2_bias: float32 [1024], P(('fsdp', 'tensor')), may hold values from -3 to 3
- fc_weight: bfloat16 [1024, 4096], P('fsdp', 'tensor'), may hold values from -0.1875 to 0.1875
- fc_bias: bfloat16 [64, 64], P('tensor', 'fsdp'), may hold values from -3 to 3
- proj_weight: bfloat16 [4096, 1024], P('tensor', 'fsdp'), may hold values from -0.09375 to 0.09375
- proj_bias: float32 [1024], P(('fsdp', 'tensor')), may hold values from -3 to 3
- out_grad: bfloat16 [24576, 1024], P(('replica', 'fsdp', 'tensor')), may hold values from -6 to 6
Outputs:
- output: float32 [24576, 1024], P(('replica', 'fsdp', 'tensor'))
- input_grad: float32 [24576, 1024], P(('replica', 'fsdp', 'tensor'))
- grad_ln1_gain: float32 [1024], P(('fsdp', 'tensor'))
- grad_ln1_bias: float32 [1024], P(('fsdp', 'tensor'))
- grad_qkv_weight: float32 [1024, 3, 1024], P('fsdp', None, 'tensor')
- grad_qv_bias: float32 [2, 16, 64], P(None, 'tensor', 'fsdp')
- grad_out_weight: float32 [1024, 1024], P('tensor', 'fsdp')
- grad_out_bias: float32 [1024], P(('fsdp', 'tensor'))
- grad_ln2_gain: float32 [1024], P(('fsdp', 'tensor'))
- grad_ln2_bias: float32 [1024], P(('fsdp', 'tensor'))
- grad_fc_weight: float32 [1024, 4096], P('fsdp', 'tensor')
- grad_fc_bias: float32 [64, 64], P('tensor', 'fsdp')
- grad_proj_weight: float32 [4096, 1024], P('tensor', 'fsdp')
- grad_proj_bias: float32 [1024], P(('fsdp', 'tensor'))
The draws below stay inside these ranges and needn't reach their ends.
All inputs are finite; a program needn't handle non-finite values.
Results may differ from the reference program's by a relative error of at most 0.014.
Values may be sent and summed in bfloat16 or wider, within the bound.
A program may use at most 192 MiB of HBM per device.

```python
import jax
import jax.numpy as jnp
from jax import lax

D = 1024
HEADS = 16
HD = 64
FF = 4096
LEN = 1024
SEQ_GRP = 3
TOK_GRP = 3072
TOKENS = 24576
N_REPLICA = 2
N_FSDP = 4


def steps_of(stream_key, dims, cuts, smallest, high):
    def one(dim, parts):
        draws = jax.random.uniform(jax.random.fold_in(jax.random.fold_in(stream_key, 6), dim), (parts,), jnp.float32, smallest / len(cuts), high / len(cuts))
        return jnp.repeat(jnp.exp(draws), dims[dim] // parts).reshape((-1,) + (1,) * (len(dims) - dim - 1))

    loudness = one(*cuts[0])
    for cut in cuts[1:]:
        loudness = loudness * one(*cut)
    return loudness


def bell_draw(own_key, shape, deviation, reach, cuts=(), held_as=jnp.bfloat16):
    array = deviation * jax.random.normal(own_key, shape, jnp.float32)
    if cuts:
        array = array * steps_of(own_key, shape, cuts, -0.22, 0.18)
    return jnp.clip(array, -reach, reach).astype(held_as)


def setup_inputs(seed: int = 0) -> dict:
    splits = jax.random.split(jax.random.key(seed), 15)
    return {
        "tokens": bell_draw(splits[0], (TOKENS, D), 1.0, 6.0, ((0, 32),)),
        "ln1_gain": jnp.clip(1.0 + 0.1 * jax.random.normal(splits[1], (D,), jnp.float32), 0.5, 1.5),
        "ln1_bias": bell_draw(splits[2], (D,), 0.5, 3.0, ((0, 16),), jnp.float32),
        "qkv_weight": bell_draw(splits[3], (D, 3, D), D ** -0.5, 0.1875, ((0, 4), (2, 4))),
        "qv_bias": bell_draw(splits[4], (2, HEADS, HD), 0.5, 3.0, ((1, 4), (2, 4))),
        "out_weight": bell_draw(splits[5], (D, D), (D // 16) ** -0.5, 0.75, ((0, 4), (1, 4))),
        "out_bias": bell_draw(splits[6], (D,), 0.5, 3.0, ((0, 16),), jnp.float32),
        "ln2_gain": jnp.clip(1.0 + 0.1 * jax.random.normal(splits[7], (D,), jnp.float32), 0.5, 1.5),
        "ln2_bias": bell_draw(splits[8], (D,), 0.5, 3.0, ((0, 16),), jnp.float32),
        "fc_weight": bell_draw(splits[9], (D, FF), D ** -0.5, 0.1875, ((0, 4), (1, 4))),
        "fc_bias": bell_draw(splits[10], (FF // HD, HD), 0.5, 3.0, ((0, 4), (1, 4))),
        "proj_weight": bell_draw(splits[11], (FF, D), FF ** -0.5, 0.09375, ((0, 4), (1, 4))),
        "proj_bias": bell_draw(splits[12], (D,), 0.5, 3.0, ((0, 16),), jnp.float32),
        "out_grad": bell_draw(splits[13], (TOKENS, D), 1.0, 6.0, ((0, 32),)),
    }


EPS = 1e-05
NEG = -1e+30

@jax.custom_vjp
def low(v):
    return lax.optimization_barrier(v.astype(jnp.bfloat16)).astype(jnp.float32)

@jax.custom_vjp
def low_back(v):
    return v

def low_keep(v):
    return (low(v), None)

def low_pass(kept, grad):
    return (grad,)

def back_keep(v):
    return (v, None)

def back_low(kept, grad):
    return (low(grad),)
low.defvjp(low_keep, low_pass)
low_back.defvjp(back_keep, back_low)

def layer_norm(values, gain, bias):
    center = values - lax.optimization_barrier(jnp.mean(values, -1, keepdims=True))
    spread = lax.optimization_barrier(jnp.mean(center * center, -1, keepdims=True))
    return center * lax.rsqrt(spread + EPS) * gain + bias

def product(left, right):
    return jnp.dot(left, right, precision=lax.Precision.HIGHEST)

def attend_sequence(item):
    query, keys, values = item
    scores = jnp.einsum('qhd,khd->hqk', query, keys, precision=lax.Precision.HIGHEST) * HD ** (-0.5)
    scores = low_back(scores)
    allowed = jnp.arange(LEN)[:, None] >= jnp.arange(LEN)[None, :]
    scores = jnp.where(allowed[None], scores, NEG)
    weights = low(jax.nn.softmax(scores, axis=-1))
    return jnp.einsum('hqk,khd->qhd', weights, values, precision=lax.Precision.HIGHEST)

def group_forward(params, inputs):
    gain_one, bias_one, qkv_w, qv_b, out_w, out_b, gain_two, bias_two, fc_w, fc_b, proj_w, proj_b = params
    normed_one = low(layer_norm(inputs, gain_one, bias_one))
    query = low_back(low(product(normed_one, qkv_w[:, 0, :]) + qv_b[0].reshape(D)))
    keys = low_back(low(product(normed_one, qkv_w[:, 1, :])))
    values = low_back(low(product(normed_one, qkv_w[:, 2, :]) + qv_b[1].reshape(D)))
    grid_shape = (SEQ_GRP, LEN, HEADS, HD)
    attended = lax.map(jax.checkpoint(attend_sequence), (query.reshape(grid_shape), keys.reshape(grid_shape), values.reshape(grid_shape)))
    attended = low_back(low(attended.reshape(TOK_GRP, D)))
    branch = low_back(product(attended, out_w) + out_b)
    middle = inputs + branch
    normed_two = low(layer_norm(middle, gain_two, bias_two))
    before = low_back(product(normed_two, fc_w) + fc_b.reshape(FF))
    activated = low(jax.nn.gelu(before, approximate=True))
    return middle + product(activated, proj_w) + proj_b

def reference(tokens, ln1_gain, ln1_bias, qkv_weight, qv_bias, out_weight, out_bias, ln2_gain, ln2_bias, fc_weight, fc_bias, proj_weight, proj_bias, out_grad):
    params = tuple((arr.astype(jnp.float32) for arr in (ln1_gain, ln1_bias, qkv_weight, qv_bias, out_weight, out_bias, ln2_gain, ln2_bias, fc_weight, fc_bias, proj_weight, proj_bias)))
    groups = N_REPLICA * N_FSDP
    inputs = tokens.astype(jnp.float32).reshape(groups, TOK_GRP, D)
    grads_in = out_grad.astype(jnp.float32).reshape(groups, TOK_GRP, D)

    def one_group(totals, item):
        rows, cotangent = item
        result, pull = jax.vjp(group_forward, params, rows)
        grad_params, grad_rows = pull(cotangent)
        totals = jax.tree.map(jnp.add, totals, grad_params)
        return (totals, (result, grad_rows))
    zeros = jax.tree.map(jnp.zeros_like, params)
    totals, (results, grad_rows) = lax.scan(one_group, zeros, (inputs, grads_in))
    return (results.reshape(TOKENS, D), grad_rows.reshape(TOKENS, D), totals[0], totals[1], totals[2], totals[3], totals[4], totals[5], totals[6], totals[7], totals[8], totals[9], totals[10], totals[11])
```

```python
import jax
import jax.numpy as jnp
from jax import lax
from jax.experimental import pallas as pl
from jax.experimental.pallas import tpu as pltpu
from jax.sharding import PartitionSpec as P

HD = 64
LEN = 1024


EPS = 1e-05
NEG = -1e30
BLOCK = 256
BF = jnp.bfloat16
F32 = jnp.float32


def dot(left, right, dims):
    return lax.dot_general(left, right, (dims, ((), ())), preferred_element_type=F32)


def mm(left, right):
    return dot(left, right, ((1,), (0,)))


def mm_t(left, right):
    return dot(left, right, ((1,), (1,)))


def t_mm(left, right):
    return dot(left, right, ((0,), (0,)))


def layer_norm(values, gain, bias):
    center = values - jnp.mean(values, -1, keepdims=True)
    spread = jnp.mean(center * center, -1, keepdims=True)
    return center * lax.rsqrt(spread + EPS) * gain + bias


def gelu_tanh(values):
    return jax.nn.gelu(values, approximate=True)


def swap(value, bit):
    size = lax.axis_size("tensor")
    return lax.ppermute(value, "tensor", [(i, i ^ bit) for i in range(size)])


def after(value, *others):
    return lax.optimization_barrier((value,) + others)[0]


def chunk_count():
    size = lax.axis_size("tensor")
    return 4 if size == 4 else 1


def gather_rows(local):
    if chunk_count() == 1:
        return [lax.all_gather(local, "tensor", axis=0, tiled=True)]
    sib = swap(local, 1)
    far = swap(local, 2)
    return [local, sib, far, swap(far, 1)]


def sum_rows(part):
    if chunk_count() == 1:
        return lax.psum_scatter(part(0), "tensor", scatter_dimension=0, tiled=True)
    side = swap(part(3).astype(BF), 1)
    cross = swap((part(2) + side.astype(F32)).astype(BF), 2)
    near = swap(part(1).astype(BF), 1)
    return part(0) + near.astype(F32) + cross.astype(F32)


def take_rows(full, k):
    if chunk_count() == 1:
        return full
    rows = full.shape[0] // 4
    return lax.dynamic_slice_in_dim(full, (lax.axis_index("tensor") ^ k) * rows, rows, 0)


def in_order(pieces):
    if len(pieces) == 1:
        return pieces[0]
    rows = pieces[0].shape[0]
    me = lax.axis_index("tensor")
    full = jnp.zeros((4 * rows, pieces[0].shape[1]), pieces[0].dtype)
    for k, piece in enumerate(pieces):
        full = lax.dynamic_update_slice_in_dim(full, piece, (me ^ k) * rows, 0)
    return full


def joined_rows(pieces):
    return pieces[0] if len(pieces) == 1 else jnp.concatenate(pieces, 0)


def replica_sum(value):
    size = lax.axis_size("replica")
    if size == 2:
        return value.astype(F32) + lax.ppermute(value, "replica", [(0, 1), (1, 0)]).astype(F32)
    return lax.psum(value, "replica").astype(F32)


def scores_t(qkv_ref, width, head, block):
    stop = (block + 1) * BLOCK
    low = head * HD
    query = qkv_ref[block * BLOCK : stop, low : low + HD]
    keys = qkv_ref[0:stop, width + low : width + low + HD]
    scores = mm_t(keys, query * jnp.asarray(HD ** (-0.5), BF))
    shape = (BLOCK, BLOCK)
    keep = lax.broadcasted_iota(jnp.int32, shape, 0) <= lax.broadcasted_iota(jnp.int32, shape, 1)
    edge = jnp.where(keep, scores[stop - BLOCK :], NEG)
    scores = edge if block == 0 else jnp.concatenate([scores[: stop - BLOCK], edge], 0)
    expo = jnp.exp(scores - jnp.max(scores, 0, keepdims=True))
    return query, keys, expo, 1.0 / jnp.sum(expo, 0, keepdims=True)


def attend_kernel(qkv_ref, out_ref):
    width = out_ref.shape[1]
    for pair in range(width // (2 * HD)):
        for block in range(LEN // BLOCK):
            stop = (block + 1) * BLOCK
            halves = []
            for head in (2 * pair, 2 * pair + 1):
                _, _, expo, inverse = scores_t(qkv_ref, width, head, block)
                low = 2 * width + head * HD
                values = qkv_ref[0:stop, low : low + HD]
                halves.append(t_mm(values, expo.astype(BF)) * inverse)
            out_ref[block * BLOCK : stop, pair * 2 * HD : (pair + 1) * 2 * HD] = (
                jnp.concatenate(halves, 0).T.astype(BF)
            )


def attend_back_kernel(qkv_ref, grad_ref, out_ref, keys_sum, values_sum):
    width = grad_ref.shape[1]
    scale = HD ** (-0.5)
    for pair in range(width // (2 * HD)):
        for block in reversed(range(LEN // BLOCK)):
            stop = (block + 1) * BLOCK
            halves = []
            for side in (0, 1):
                head = 2 * pair + side
                query, keys, expo, inverse = scores_t(qkv_ref, width, head, block)
                low = head * HD
                values = qkv_ref[0:stop, 2 * width + low : 2 * width + low + HD]
                grad = grad_ref[block * BLOCK : stop, low : low + HD]
                probs = expo * inverse
                grad_values = mm(probs.astype(BF), grad)
                grad_probs = mm_t(values, grad)
                weighted = probs * grad_probs
                total = jnp.sum(weighted, 0, keepdims=True)
                grad_scores = (weighted - probs * total).astype(BF)
                grad_keys = mm(grad_scores, query)
                lanes = slice(side * HD, (side + 1) * HD)
                if stop == LEN:
                    values_sum[:, lanes] = grad_values
                    keys_sum[:, lanes] = grad_keys
                else:
                    values_sum[0:stop, lanes] += grad_values
                    keys_sum[0:stop, lanes] += grad_keys
                halves.append(t_mm(keys, grad_scores))
            low = pair * 2 * HD
            out_ref[block * BLOCK : stop, low : low + 2 * HD] = (
                jnp.concatenate(halves, 0).T * scale
            ).astype(BF)
        out_ref[:, width + low : width + low + 2 * HD] = (keys_sum[...] * scale).astype(BF)
        out_ref[:, 2 * width + low : 2 * width + low + 2 * HD] = values_sum[...].astype(BF)


def rows_spec(width):
    return pl.BlockSpec((LEN, width), lambda i: (i, 0))


def attend(qkv):
    rows, width = qkv.shape[0], qkv.shape[1] // 3
    return pl.pallas_call(
        attend_kernel,
        grid=(rows // LEN,),
        in_specs=[rows_spec(3 * width)],
        out_specs=rows_spec(width),
        out_shape=jax.ShapeDtypeStruct((rows, width), BF),
        cost_estimate=pl.CostEstimate(
            flops=24_000_000_000, bytes_accessed=8 * rows * width, transcendentals=rows * width * 4
        ),
        compiler_params=pltpu.CompilerParams(vmem_limit_bytes=48 * 1024 * 1024),
        name="attend",
    )(qkv)


def attend_back(qkv, grad):
    rows, width = grad.shape
    return pl.pallas_call(
        attend_back_kernel,
        grid=(rows // LEN,),
        in_specs=[rows_spec(3 * width), rows_spec(width)],
        out_specs=rows_spec(3 * width),
        out_shape=jax.ShapeDtypeStruct((rows, 3 * width), BF),
        scratch_shapes=[pltpu.VMEM((LEN, 2 * HD), F32), pltpu.VMEM((LEN, 2 * HD), F32)],
        cost_estimate=pl.CostEstimate(
            flops=48_000_000_000, bytes_accessed=14 * rows * width, transcendentals=rows * width * 4
        ),
        compiler_params=pltpu.CompilerParams(vmem_limit_bytes=48 * 1024 * 1024),
        name="attend_back",
    )(qkv, grad)


def pack(flat):
    size = flat.shape[-1]
    full = -(-size // 1024) * 1024
    flat = jnp.pad(flat, [(0, 0)] * (flat.ndim - 1) + [(0, full - size)])
    return flat.reshape(flat.shape[:-1] + (full // 128, 128))


def on_device(
    tokens,
    ln1_gain,
    ln1_bias,
    qkv_weight,
    qv_bias,
    out_weight,
    out_bias,
    ln2_gain,
    ln2_bias,
    fc_weight,
    fc_bias,
    proj_weight,
    proj_bias,
    out_grad,
):
    both = ("fsdp", "tensor")
    n_fsdp, n_tensor = lax.axis_size("fsdp"), lax.axis_size("tensor")
    me = lax.axis_index("tensor")
    part = ln1_gain.shape[0]
    width = out_weight.shape[0]
    heads = width // HD
    hidden = fc_weight.shape[1]
    model = tokens.shape[1]
    vectors = jnp.concatenate(
        [
            ln1_gain,
            ln1_bias,
            ln2_gain,
            ln2_bias,
            out_bias,
            proj_bias,
            qv_bias.astype(F32).reshape(-1),
            fc_bias.astype(F32).reshape(-1),
        ]
    )
    bundle = lax.all_gather(pack(vectors), both, axis=0, tiled=False)
    bundle = bundle.reshape(n_fsdp * n_tensor, -1)
    gain_one, bias_one, gain_two, bias_two, bias_out, bias_proj = (
        bundle[:, i * part : (i + 1) * part].reshape(-1) for i in range(6)
    )
    mine = lax.dynamic_index_in_dim(bundle.reshape(n_fsdp, n_tensor, -1), me, 1, keepdims=False)
    low, high = 6 * part, 6 * part + qv_bias.size
    qv_full = (
        mine[:, low:high].reshape((n_fsdp,) + qv_bias.shape).transpose(1, 2, 0, 3).reshape(2, width)
    )
    fcb_full = (
        mine[:, high : high + fc_bias.size]
        .reshape((n_fsdp,) + fc_bias.shape)
        .transpose(1, 0, 2)
        .reshape(hidden)
    )
    bias_row = jnp.concatenate([qv_full[0], jnp.zeros((width,), F32), qv_full[1]])
    joined = lax.all_gather(
        qkv_weight.reshape(qkv_weight.shape[0], 3 * width), "fsdp", axis=0, tiled=True
    )
    out_full = lax.all_gather(out_weight, "fsdp", axis=1, tiled=True)
    fc_full = lax.all_gather(fc_weight, "fsdp", axis=0, tiled=True)
    proj_full = lax.all_gather(proj_weight, "fsdp", axis=1, tiled=True)

    inputs = tokens.astype(F32)
    normed_one = gather_rows(layer_norm(inputs, gain_one, bias_one).astype(BF))
    qkv = in_order([(mm(piece, joined) + bias_row).astype(BF) for piece in normed_one])
    attended = attend(qkv)
    att = [take_rows(attended, k) for k in range(chunk_count())]
    grads = gather_rows(after(out_grad, qkv))
    middle = inputs + (sum_rows(lambda k: mm(att[k], out_full)) + bias_out)
    normed_two = gather_rows(layer_norm(middle, gain_two, bias_two).astype(BF))
    before = [mm(piece, fc_full) + fcb_full for piece in normed_two]
    act = [gelu_tanh(piece).astype(BF) for piece in before]

    grad_pre = []
    for piece, grad in zip(before, grads):
        pull = jax.vjp(gelu_tanh, piece)[1]
        grad_pre.append(pull(mm_t(grad, proj_full))[0].astype(BF))
    grad_normed_two = sum_rows(lambda k: mm_t(grad_pre[k], fc_full))
    grad_pre_all = joined_rows(grad_pre)
    grad_proj = t_mm(joined_rows(act), joined_rows(grads)).astype(BF)
    grad_fc = t_mm(joined_rows(normed_two), grad_pre_all).astype(BF)
    grad_fc_bias = jnp.sum(grad_pre_all, 0, dtype=F32)
    grad_proj_bias = jnp.sum(out_grad, 0, dtype=F32)
    norm_pull_two = jax.vjp(layer_norm, middle, gain_two, bias_two)[1]
    grad_middle_part, grad_gain_two, grad_bias_two = norm_pull_two(grad_normed_two)
    grad_middle = out_grad.astype(F32) + grad_middle_part
    grad_branch = grad_middle.astype(BF)
    grad_out_bias = jnp.sum(grad_branch, 0, dtype=F32)
    branches = gather_rows(grad_branch)
    grad_attended = in_order([mm_t(piece, out_full).astype(BF) for piece in branches])

    late = lax.optimization_barrier((grad_attended, *act))
    grad_attended, act = late[0], late[1:]
    output = middle + sum_rows(lambda k: mm(act[k], proj_full)) + bias_proj
    grad_qkv = attend_back(qkv, grad_attended)
    grad_out = t_mm(joined_rows(att), joined_rows(branches)).astype(BF)
    pieces = [take_rows(grad_qkv, k) for k in range(chunk_count())]
    grad_normed_one = sum_rows(lambda k: mm_t(pieces[k], joined))
    pieces_all = joined_rows(pieces)
    grad_joined = t_mm(joined_rows(normed_one), pieces_all).astype(BF)
    qkv_sums = jnp.sum(pieces_all, 0, dtype=F32)
    norm_pull_one = jax.vjp(layer_norm, inputs, gain_one, bias_one)[1]
    grad_input_part, grad_gain_one, grad_bias_one = norm_pull_one(grad_normed_one)
    input_grad = grad_middle + grad_input_part

    def scatter(value, dim):
        return replica_sum(
            lax.psum_scatter(value, "fsdp", scatter_dimension=dim, tiled=True).astype(BF)
        )

    total_proj = scatter(grad_proj, 1)
    total_fc = scatter(grad_fc, 0)
    total_out = scatter(grad_out, 1)
    total_joined = scatter(grad_joined, 0)

    wide = jnp.stack(
        [grad_gain_one, grad_bias_one, grad_gain_two, grad_bias_two, grad_out_bias, grad_proj_bias]
    )
    wide = wide.reshape(6, n_fsdp * n_tensor, part).transpose(1, 0, 2).reshape(-1, 6 * part)
    grad_qv = jnp.stack([qkv_sums[:width], qkv_sums[2 * width :]])
    grad_qv = grad_qv.reshape(2, heads, n_fsdp, -1).transpose(2, 0, 1, 3).reshape(n_fsdp, -1)
    grad_fcb = grad_fc_bias.reshape(fc_bias.shape[0], n_fsdp, -1).transpose(1, 0, 2)
    own = jnp.concatenate([grad_qv, grad_fcb.reshape(n_fsdp, -1)], -1)
    is_me = (jnp.arange(n_tensor, dtype=jnp.int32) == me)[None, :, None]
    own = jnp.where(is_me, own[:, None, :], 0.0).reshape(n_fsdp * n_tensor, -1)
    sums = lax.psum_scatter(
        pack(jnp.concatenate([wide, own], -1)), both, scatter_dimension=0, tiled=False
    )
    sums = replica_sum(sums).reshape(-1)
    vec = [sums[i * part : (i + 1) * part] for i in range(6)]
    total_qv = sums[low:high].reshape(qv_bias.shape)
    total_fcb = sums[high : high + fc_bias.size].reshape(fc_bias.shape)
    return (
        output,
        input_grad,
        vec[0],
        vec[1],
        total_joined.reshape(qkv_weight.shape),
        total_qv,
        total_out,
        vec[4],
        vec[2],
        vec[3],
        total_fc,
        total_fcb,
        total_proj,
        vec[5],
    )


def solution(mesh):
    placed = (
        P(("replica", "fsdp", "tensor"), None),
        P(("fsdp", "tensor")),
        P(("fsdp", "tensor")),
        P("fsdp", None, "tensor"),
        P(None, "tensor", "fsdp"),
        P("tensor", "fsdp"),
        P(("fsdp", "tensor")),
        P(("fsdp", "tensor")),
        P(("fsdp", "tensor")),
        P("fsdp", "tensor"),
        P("tensor", "fsdp"),
        P("tensor", "fsdp"),
        P(("fsdp", "tensor")),
        P(("replica", "fsdp", "tensor"), None),
    )
    return jax.shard_map(
        on_device,
        mesh=mesh,
        in_specs=placed,
        out_specs=(
            P(("replica", "fsdp", "tensor"), None),
            P(("replica", "fsdp", "tensor"), None),
            P(("fsdp", "tensor")),
            P(("fsdp", "tensor")),
            P("fsdp", None, "tensor"),
            P(None, "tensor", "fsdp"),
            P("tensor", "fsdp"),
            P(("fsdp", "tensor")),
            P(("fsdp", "tensor")),
            P(("fsdp", "tensor")),
            P("fsdp", "tensor"),
            P("tensor", "fsdp"),
            P("tensor", "fsdp"),
            P(("fsdp", "tensor")),
        ),
        check_vma=False,
    )
```
